32 devices in a mesh: virt: 8 (over y, x, core), occ: 4 (over z).
Axes of the slice: x: 2, y: 2, z: 4, core: 2. Of those that a mesh axis runs over, the one named last changes fastest.
Arguments:
- amplitudes: bfloat16 [512, 4096], P('occ', 'virt'), may hold values from -6 to 6
- integrals: bfloat16 [1024, 16384], P(None, 'virt'), may hold values from -0.1875 to 0.1875
- panel_owner: int32 [4, 2], P('occ'), may hold values from 0 to 7, as said below
- inter: bfloat16 [8192, 8192], P('occ', 'virt'), may hold values from -0.125 to 0.125
- dest: int32 [4, 8, 16], P('occ', 'virt'), may hold values from 0 to 3, as said below
- screen: int32 [4, 8, 16], P('occ', 'virt'), may hold values from 0 to 1
Outputs:
- contracted: bfloat16 [512, 8192], P('occ', 'virt')
The draws below stay inside these ranges and needn't reach their ends.
Inputs may be any that keep to these rules, and one draw needn't show every extreme that they name: `panel_owner`: in each row the 2 entries are distinct. `dest`: among the subtiles of one device that screen marks 1, no two name the same owner.
All inputs are finite; a program needn't handle non-finite values.
Results may differ from the reference program's by a relative error of at most 0.0055.
Values may be sent and summed in bfloat16 or wider, within the bound.
A program may use at most 64 MiB of HBM per device.

```python
import jax
import jax.numpy as jnp
from jax import lax

TILE = 512
CT = 4
SROWS = 32
HALVES = 4
WCOLS = 1024
STEPS = 2
COLS = 2048
OP = 128
SUB = 16
KWIN = 1024
AROWS = 512
ACOLS = 4096
VCOLS = 16384
WROWS = 8192
OCOLS = 8192
N_VIRT = 8
N_OCC = 4


def draw_panel_owner(key, part):
    noise = jax.random.randint(jax.random.fold_in(key, 101), (N_OCC, N_VIRT), 0, 1 << 20)
    score = noise * N_VIRT + jnp.arange(N_VIRT, dtype=jnp.int32)[None, :]
    first = jax.random.randint(jax.random.fold_in(key, 102), (), 0, N_OCC)
    other = (first + 1 + jax.random.randint(jax.random.fold_in(key, 103), (), 0, N_OCC - 1)) % N_OCC
    score = score.at[first, N_VIRT - 1].set(-2)
    score = score.at[other, 0].set(-1)
    order = jnp.argsort(score, axis=1)[:, :STEPS]
    return order.astype(jnp.int32)


def route_tables(key):
    bias = jax.random.randint(jax.random.fold_in(key, 201), (N_OCC,), 0, 4 * N_OCC)
    noise = jax.random.randint(jax.random.fold_in(key, 202), (N_OCC, N_VIRT, N_OCC), 0, 4 * N_OCC)
    score = (noise + bias[None, None, :]) * N_OCC + jnp.arange(N_OCC, dtype=jnp.int32)[None, None, :]
    score = score.at[0, 0, N_OCC - 1].set(-2)
    score = score.at[0, 0, 0].set(-1)
    ranked = jnp.argsort(score, axis=2)
    slot_index = jnp.arange(SUB, dtype=jnp.int32)
    owners = jnp.take(ranked, slot_index % N_OCC, axis=2).astype(jnp.int32)
    coin = jax.random.randint(jax.random.fold_in(key, 203), (N_OCC, N_VIRT, SUB), 0, 4)
    live = ((coin > 0) & (slot_index[None, None, :] < N_OCC)).astype(jnp.int32)
    live = live.at[0, 0, 0].set(1)
    live = live.at[0, 0, 1].set(1)
    return (owners, live)


def draw_dest(key, part):
    return route_tables(key)[0]


def draw_screen(key, part):
    return route_tables(key)[1]


def block_scale(stream_key, extent, pieces, least, top_value):
    gain, own = 1.0, jax.random.fold_in(stream_key, 6)
    for position, shards_of in pieces:
        steps = jnp.exp(jax.random.uniform(jax.random.fold_in(own, position), (shards_of,), jnp.float32, least / len(pieces), top_value / len(pieces)))
        gain = gain * jnp.repeat(steps, extent[position] // shards_of).reshape([-1 if axis == position else 1 for axis in range(len(extent))])
    return gain


def scatter_about(stream_key, extent, scale, reach, cuts=(), held_as=jnp.bfloat16):
    array = scale * jax.random.normal(stream_key, extent, jnp.float32)
    if cuts:
        array = array * block_scale(stream_key, extent, cuts, -0.22, 0.18)
    return jnp.clip(array, -reach, reach).astype(held_as)


def setup_inputs(seed: int = 0) -> dict:
    seeds = jax.random.split(jax.random.key(seed), 7)
    return {
        "amplitudes": scatter_about(seeds[0], (AROWS, ACOLS), 1.0, 6.0, ((0, 4), (1, 8))),
        "integrals": scatter_about(seeds[1], (KWIN, VCOLS), KWIN ** -0.5, 0.1875, ((1, 8),)),
        "panel_owner": draw_panel_owner(jax.random.fold_in(seeds[6], 71), 0),
        "inter": scatter_about(seeds[3], (WROWS, OCOLS), COLS ** -0.5, 0.125, ((0, 4), (1, 8))),
        "dest": draw_dest(jax.random.fold_in(seeds[6], 71), 0),
        "screen": draw_screen(jax.random.fold_in(seeds[6], 71), 0),
    }


def reference(amplitudes, integrals, panel_owner, inter, dest, screen):
    def one_group(g):
        rows = lax.dynamic_slice_in_dim(amplitudes, (g * OP).astype(jnp.int32), OP, 0)
        rows = rows.reshape(OP, N_VIRT, TILE)
        owners = lax.dynamic_index_in_dim(panel_owner, g, 0, keepdims=False)
        amplitude_panels = jnp.take(rows, owners, axis=1).reshape(OP, KWIN)
        return jnp.dot(amplitude_panels, integrals, preferred_element_type=jnp.float32).astype(jnp.bfloat16)

    ladder = lax.map(one_group, jnp.arange(N_OCC, dtype=jnp.int32))
    subtiles = ladder.reshape(N_OCC, HALVES, SROWS, N_VIRT, CT, TILE)
    subtiles = subtiles.transpose(0, 3, 1, 4, 2, 5).reshape(N_OCC, N_VIRT, SUB, SROWS, TILE)

    def one_owner(o):
        weight = ((dest == o) & (screen == 1)).astype(jnp.float32)

        def accumulate_group_sum(total, g):
            part = subtiles[g].astype(jnp.float32) * weight[g][:, :, None, None]
            return total + part, None

        start = jnp.zeros((N_VIRT, SUB, SROWS, TILE), jnp.float32)
        total, _ = lax.scan(accumulate_group_sum, start, jnp.arange(N_OCC, dtype=jnp.int32))
        gathered = total.astype(jnp.bfloat16)
        left = gathered.reshape(N_VIRT, HALVES, CT, SROWS, TILE).transpose(0, 1, 3, 2, 4).reshape(N_VIRT, OP, COLS)
        block = lax.dynamic_slice_in_dim(inter, (o * COLS).astype(jnp.int32), COLS, 0).reshape(COLS, N_VIRT, WCOLS)
        result = jnp.einsum("vrk,kvw->rvw", left.astype(jnp.float32), block.astype(jnp.float32))
        return result.reshape(OP, N_VIRT * WCOLS).astype(jnp.bfloat16)

    outs = lax.map(one_owner, jnp.arange(N_OCC, dtype=jnp.int32))
    return outs.reshape(N_OCC * OP, N_VIRT * WCOLS)
```

```python
import functools

import jax
import jax.numpy as jnp
from jax import lax
from jax.experimental import pallas as pl
from jax.experimental.pallas import tpu as pltpu
from jax.sharding import PartitionSpec as P

SROWS = 32
MESH = pl.DeviceIdType.MESH


def flip(index, bit):
    return index + bit * (1 - 2 * lax.rem(lax.div(index, bit), 2))


def peer(me, j, n):
    up = lax.div(me, (n + 1) // 2)
    rising = j + lax.div(j - me + n, n)
    falling = n - 1 - j
    falling = falling - lax.div(me - falling + n, n)
    return up * rising + (1 - up) * falling


def kernel(
    n_virt, n_occ, dims,
    owner_ref, dest_ref, screen_ref, amp_hbm, integ_hbm, inter_hbm,
    out_ref,
    held, integ, inter, route, tables, leaving, arrived, total,
    amp_sem, integ_sem, inter_sem,
    chip_send, chip_recv, pair_send, pair_recv,
    table_send, table_recv, tile_send, tile_recv,
):
    v = lax.axis_index("virt")
    g = lax.axis_index("occ")
    n_chips = n_virt // 2
    chip, core = lax.div(v, 2), lax.rem(v, 2)
    pair = flip(v, 1)
    halves, tile = held.shape[1], held.shape[3]
    steps = owner_ref.shape[1]
    n_sub = dest_ref.shape[2]
    col_tiles = integ.shape[0]

    amp_copy = pltpu.make_async_copy(amp_hbm, held.at[v], amp_sem)
    amp_copy.start()

    barrier = pltpu.get_barrier_semaphore()
    pl.semaphore_signal(barrier, inc=1, device_id={"virt": pair}, device_id_type=MESH)
    for d in range(dims):
        near = flip(chip, 1 << d) * 2 + core
        pl.semaphore_signal(barrier, inc=1, device_id={"virt": near}, device_id_type=MESH)
    for j in range(n_occ - 1):
        pl.semaphore_signal(
            barrier, inc=1, device_id={"occ": peer(g, j, n_occ)}, device_id_type=MESH
        )

    integ_copies, inter_copies = [], []
    for c in range(col_tiles):
        part = integ_hbm.at[:, pl.ds(c * tile, tile)]
        integ_copies.append(pltpu.make_async_copy(part, integ.at[c], integ_sem.at[c]))
        integ_copies[-1].start()
    for c in range(col_tiles):
        part = inter_hbm.at[pl.ds(c * tile, tile)]
        inter_copies.append(pltpu.make_async_copy(part, inter.at[c], inter_sem.at[c]))
        inter_copies[-1].start()

    named = jnp.where(screen_ref[0] == 1, dest_ref[0], -1)
    route[...] = jnp.full(route.shape, -1, jnp.int32)
    route[0:1, 0:n_sub] = named
    label = lax.broadcasted_iota(jnp.int32, (1, n_sub), 1) + 1

    amp_copy.wait()
    pl.semaphore_wait(barrier, 1 + dims + n_occ - 1)

    part_halves = halves // dims

    def chunk(p, rel, bit_core):
        source = chip
        for d in range(dims):
            if rel >> d & 1:
                source = flip(source, 1 << d)
        return held.at[source * 2 + bit_core, pl.ds(p * part_halves, part_halves)]

    def chip_copy(p, rel, d):
        ref = chunk(p, rel, core)
        got = rel ^ (1 << d)
        return pltpu.make_async_remote_copy(
            src_ref=ref, dst_ref=ref,
            send_sem=chip_send.at[p, got], recv_sem=chip_recv.at[p, got],
            device_id={"virt": flip(chip, 1 << d) * 2 + core}, device_id_type=MESH,
        )

    def pair_copy(p, rel):
        ref = chunk(p, rel, core)
        return pltpu.make_async_remote_copy(
            src_ref=ref, dst_ref=ref,
            send_sem=pair_send.at[p, rel], recv_sem=pair_recv.at[p, rel],
            device_id={"virt": pair}, device_id_type=MESH,
        )

    orders = [[(p + t) % dims for t in range(dims)] for p in range(dims)]
    crossing, pairing = {}, {}

    def send_on(p, rel, first):
        for t in range(first, dims):
            d = orders[p][t]
            copy = chip_copy(p, rel, d)
            copy.start()
            crossing[p, rel ^ (1 << d)] = (copy, t + 1)

    for t in range(dims):
        for p in range(dims):
            d = orders[p][t]
            copy = chip_copy(p, 0, d)
            copy.start()
            crossing[p, 1 << d] = (copy, t + 1)
    for p in range(dims):
        pairing[p, 0] = pair_copy(p, 0)
        pairing[p, 0].start()

    table_copies = []
    for j in range(n_occ - 1):
        copy = pltpu.make_async_remote_copy(
            src_ref=route, dst_ref=tables.at[g],
            send_sem=table_send.at[j], recv_sem=table_recv.at[g],
            device_id={"occ": peer(g, j, n_occ)}, device_id_type=MESH,
        )
        copy.start()
        table_copies.append(copy)

    done = set()
    for depth in range(1, dims + 1):
        for p in range(dims):
            for key in [k for k in crossing if k[0] == p and crossing[k][1] == depth and k not in done]:
                copy, after = crossing[key]
                copy.wait_recv()
                done.add(key)
                send_on(key[0], key[1], after)
                pairing[key] = pair_copy(*key)
                pairing[key].start()

    for key in pairing:
        pairing[key].wait_recv()

    for copy in integ_copies:
        copy.wait()

    def made(owner):
        k1 = jnp.sum(jnp.where(named == owner, label, 0))
        k = jnp.maximum(k1 - 1, 0)
        h, c = lax.div(k, col_tiles), lax.rem(k, col_tiles)
        acc = jnp.zeros((SROWS, tile), jnp.float32)
        for s in range(steps):
            left = held[owner_ref[0, s], h]
            right = integ[c, pl.ds(s * tile, tile), :]
            acc += jnp.dot(left, right, preferred_element_type=jnp.float32)
        return jnp.where(k1 > 0, acc, 0.0).astype(jnp.bfloat16)

    tile_copies = []
    for j in range(n_occ - 1):
        owner = peer(g, j, n_occ)
        leaving[j] = made(owner)
        copy = pltpu.make_async_remote_copy(
            src_ref=leaving.at[j], dst_ref=arrived.at[g],
            send_sem=tile_send.at[j], recv_sem=tile_recv.at[g],
            device_id={"occ": owner}, device_id_type=MESH,
        )
        copy.start()
        tile_copies.append(copy)

    for copy in inter_copies:
        copy.wait()

    def add(subtile, table, first):
        k = jnp.maximum(jnp.sum(jnp.where(table == g, label, 0)) - 1, 0)
        h, c = lax.div(k, col_tiles), lax.rem(k, col_tiles)
        part = jnp.dot(subtile, inter[c], preferred_element_type=jnp.float32)
        for i in range(halves):
            rows = pl.ds(i * SROWS, SROWS)
            term = jnp.where(h == i, part, 0.0)
            total[rows] = term if first else total[rows] + term

    add(made(g), named, True)
    for j in reversed(range(n_occ - 1)):
        source = peer(g, j, n_occ)
        pltpu.make_async_remote_copy(
            src_ref=route, dst_ref=tables.at[source],
            send_sem=table_send.at[j], recv_sem=table_recv.at[source],
            device_id={"occ": source}, device_id_type=MESH,
        ).wait_recv()
        pltpu.make_async_remote_copy(
            src_ref=leaving.at[j], dst_ref=arrived.at[source],
            send_sem=tile_send.at[j], recv_sem=tile_recv.at[source],
            device_id={"occ": source}, device_id_type=MESH,
        ).wait_recv()
        add(arrived[source], tables[source, 0:1, 0:n_sub], False)
    out_ref[...] = total[...].astype(out_ref.dtype)

    for key in crossing:
        crossing[key][0].wait_send()
    for key in pairing:
        pairing[key].wait_send()
    for copy in table_copies + tile_copies:
        copy.wait_send()


def solution(mesh):
    n_virt, n_occ = mesh.shape["virt"], mesh.shape["occ"]
    n_chips = n_virt // 2
    dims = n_chips.bit_length() - 1
    assert n_chips == 1 << dims

    def on_device(amplitudes, integrals, panel_owner, inter, dest, screen):
        op_rows, tile = amplitudes.shape
        w_cols = inter.shape[1]
        halves, col_tiles = op_rows // SROWS, integrals.shape[1] // tile
        return pl.pallas_call(
            functools.partial(kernel, n_virt, n_occ, dims),
            out_shape=jax.ShapeDtypeStruct((op_rows, w_cols), jnp.bfloat16),
            in_specs=[
                pl.BlockSpec(memory_space=pltpu.SMEM),
                pl.BlockSpec(memory_space=pltpu.VMEM),
                pl.BlockSpec(memory_space=pltpu.VMEM),
                pl.BlockSpec(memory_space=pl.ANY),
                pl.BlockSpec(memory_space=pl.ANY),
                pl.BlockSpec(memory_space=pl.ANY),
            ],
            out_specs=pl.BlockSpec(memory_space=pltpu.VMEM),
            scratch_shapes=[
                pltpu.VMEM((n_virt, halves, SROWS, tile), jnp.bfloat16),
                pltpu.VMEM((col_tiles, integrals.shape[0], tile), jnp.bfloat16),
                pltpu.VMEM((col_tiles, tile, w_cols), jnp.bfloat16),
                pltpu.VMEM((8, 128), jnp.int32),
                pltpu.VMEM((n_occ, 8, 128), jnp.int32),
                pltpu.VMEM((n_occ, SROWS, tile), jnp.bfloat16),
                pltpu.VMEM((n_occ, SROWS, tile), jnp.bfloat16),
                pltpu.VMEM((op_rows, w_cols), jnp.float32),
                pltpu.SemaphoreType.DMA,
                pltpu.SemaphoreType.DMA((col_tiles,)),
                pltpu.SemaphoreType.DMA((col_tiles,)),
                pltpu.SemaphoreType.DMA((dims, n_chips)),
                pltpu.SemaphoreType.DMA((dims, n_chips)),
                pltpu.SemaphoreType.DMA((dims, n_chips)),
                pltpu.SemaphoreType.DMA((dims, n_chips)),
                pltpu.SemaphoreType.DMA((n_occ,)),
                pltpu.SemaphoreType.DMA((n_occ,)),
                pltpu.SemaphoreType.DMA((n_occ,)),
                pltpu.SemaphoreType.DMA((n_occ,)),
            ],
            compiler_params=pltpu.CompilerParams(collective_id=0, has_side_effects=True),
        )(panel_owner, dest, screen, amplitudes.reshape(halves, SROWS, tile), integrals, inter)

    return jax.shard_map(
        on_device,
        mesh=mesh,
        in_specs=(
            P("occ", "virt"),
            P(None, "virt"),
            P("occ", None),
            P("occ", "virt"),
            P("occ", "virt", None),
            P("occ", "virt", None),
        ),
        out_specs=P("occ", "virt"),
        check_vma=False,
    )
```

```python
import functools

import jax
import jax.numpy as jnp
from jax import lax
from jax.experimental import pallas as pl
from jax.experimental.pallas import tpu as pltpu
from jax.sharding import PartitionSpec as P

SROWS = 32
MESH = pl.DeviceIdType.MESH


def flip(index, bit):
    return index + bit * (1 - 2 * lax.rem(lax.div(index, bit), 2))


def peer(me, j, n):
    up = lax.div(me, (n + 1) // 2)
    rising = j + lax.div(j - me + n, n)
    falling = n - 1 - j
    falling = falling - lax.div(me - falling + n, n)
    return up * rising + (1 - up) * falling


def kernel(
    n_virt, n_occ, dims,
    owner_hbm, dest_hbm, screen_hbm, amp_hbm, integ_hbm, inter_hbm,
    out_ref,
    owner_ref, dest_ref, screen_ref, held, integ, inter, route, tables, leaving, arrived, total,
    small_sem, amp_sem, integ_sem, inter_sem, left_sem, right_sem,
    chip_send, chip_recv, pair_send, pair_recv,
    table_send, table_recv, tile_send, tile_recv,
):
    v = lax.axis_index("virt")
    g = lax.axis_index("occ")
    n_chips = n_virt // 2
    chip, core = lax.div(v, 2), lax.rem(v, 2)
    pair = flip(v, 1)
    halves, tile = held.shape[1], held.shape[3]
    steps = owner_ref.shape[1]
    n_sub = dest_ref.shape[2]
    col_tiles = integ.shape[0]

    barrier = pltpu.get_barrier_semaphore()
    pl.semaphore_signal(barrier, inc=1, device_id={"virt": pair}, device_id_type=MESH)
    for d in range(dims):
        near = flip(chip, 1 << d) * 2 + core
        pl.semaphore_signal(barrier, inc=1, device_id={"virt": near}, device_id_type=MESH)

    def to_right(sem):
        pl.semaphore_signal(sem, inc=1, device_id={"occ": lax.rem(g + 1, n_occ)}, device_id_type=MESH)

    def to_left(sem):
        pl.semaphore_signal(sem, inc=1, device_id={"occ": lax.rem(g + n_occ - 1, n_occ)}, device_id_type=MESH)

    @pl.when(g < n_occ - 1)
    def _():
        to_right(barrier)

    @pl.when(g > 0)
    def _():
        to_left(barrier)

    amp_copy = pltpu.make_async_copy(amp_hbm, held.at[v], amp_sem)
    amp_copy.start()
    small_copies = [
        pltpu.make_async_copy(src, dst, small_sem.at[i])
        for i, (src, dst) in enumerate(
            [(dest_hbm, dest_ref), (screen_hbm, screen_ref), (owner_hbm, owner_ref)]
        )
    ]
    for copy in small_copies:
        copy.start()

    def told_send(r):
        @pl.when((g >= r - 1) & (g < n_occ - 1))
        def _():
            to_right(left_sem)

        @pl.when((g <= n_occ - r) & (g > 0))
        def _():
            to_left(right_sem)

    def told_wait(r):
        @pl.when(g >= r)
        def _():
            pl.semaphore_wait(left_sem, 1)

        @pl.when(g <= n_occ - 1 - r)
        def _():
            pl.semaphore_wait(right_sem, 1)

    integ_copies, inter_copies = [], []
    for c in range(col_tiles):
        part = integ_hbm.at[:, pl.ds(c * tile, tile)]
        integ_copies.append(pltpu.make_async_copy(part, integ.at[c], integ_sem.at[c]))
        integ_copies[-1].start()
    for c in range(col_tiles):
        part = inter_hbm.at[pl.ds(c * tile, tile)]
        inter_copies.append(pltpu.make_async_copy(part, inter.at[c], inter_sem.at[c]))
        inter_copies[-1].start()

    for copy in small_copies:
        copy.wait()
    named = jnp.where(screen_ref[0] == 1, dest_ref[0], -1)
    route[...] = jnp.full(route.shape, -1, jnp.int32)
    route[0:1, 0:n_sub] = named
    label = lax.broadcasted_iota(jnp.int32, (1, n_sub), 1) + 1

    amp_copy.wait()
    below, above = lax.div(g + n_occ - 1, n_occ), lax.div(2 * n_occ - 2 - g, n_occ)
    pl.semaphore_wait(barrier, 1 + dims + below + above)

    part_halves = halves // dims

    def chunk(p, rel, bit_core):
        source = chip
        for d in range(dims):
            if rel >> d & 1:
                source = flip(source, 1 << d)
        return held.at[source * 2 + bit_core, pl.ds(p * part_halves, part_halves)]

    def chip_copy(p, rel, d):
        ref = chunk(p, rel, core)
        got = rel ^ (1 << d)
        return pltpu.make_async_remote_copy(
            src_ref=ref, dst_ref=ref,
            send_sem=chip_send.at[p, got], recv_sem=chip_recv.at[p, got],
            device_id={"virt": flip(chip, 1 << d) * 2 + core}, device_id_type=MESH,
        )

    def pair_copy(p, rel):
        ref = chunk(p, rel, core)
        return pltpu.make_async_remote_copy(
            src_ref=ref, dst_ref=ref,
            send_sem=pair_send.at[p, rel], recv_sem=pair_recv.at[p, rel],
            device_id={"virt": pair}, device_id_type=MESH,
        )

    orders = [[(p + t) % dims for t in range(dims)] for p in range(dims)]
    crossing, pairing = {}, {}

    def send_on(p, rel, first):
        for t in range(first, dims):
            d = orders[p][t]
            copy = chip_copy(p, rel, d)
            copy.start()
            crossing[p, rel ^ (1 << d)] = (copy, t + 1)

    for t in range(dims):
        for p in range(dims):
            d = orders[p][t]
            copy = chip_copy(p, 0, d)
            copy.start()
            crossing[p, 1 << d] = (copy, t + 1)
    for p in range(dims):
        pairing[p, 0] = pair_copy(p, 0)
        pairing[p, 0].start()

    if n_occ > 2:
        told_send(2)

    done = set()
    for depth in range(1, dims + 1):
        if depth == dims:
            for r in range(2, n_occ - 1):
                told_wait(r)
                told_send(r + 1)
        for p in range(dims):
            for key in [k for k in crossing if k[0] == p and crossing[k][1] == depth and k not in done]:
                copy, after = crossing[key]
                copy.wait_recv()
                done.add(key)
                send_on(key[0], key[1], after)
                pairing[key] = pair_copy(*key)
                pairing[key].start()

    for key in pairing:
        pairing[key].wait_recv()

    for copy in integ_copies:
        copy.wait()
    if n_occ > 2:
        told_wait(n_occ - 1)

    table_copies = []
    for j in range(n_occ - 1):
        copy = pltpu.make_async_remote_copy(
            src_ref=route, dst_ref=tables.at[g],
            send_sem=table_send.at[j], recv_sem=table_recv.at[g],
            device_id={"occ": peer(g, j, n_occ)}, device_id_type=MESH,
        )
        copy.start()
        table_copies.append(copy)

    def made(owner):
        k1 = jnp.sum(jnp.where(named == owner, label, 0))
        k = jnp.maximum(k1 - 1, 0)
        h, c = lax.div(k, col_tiles), lax.rem(k, col_tiles)
        acc = jnp.zeros((SROWS, tile), jnp.float32)
        for s in range(steps):
            left = held[owner_ref[0, s], h]
            right = integ[c, pl.ds(s * tile, tile), :]
            acc += jnp.dot(left, right, preferred_element_type=jnp.float32)
        return jnp.where(k1 > 0, acc, 0.0).astype(jnp.bfloat16)

    tile_copies = []
    for j in range(n_occ - 1):
        owner = peer(g, j, n_occ)
        leaving[j] = made(owner)
        copy = pltpu.make_async_remote_copy(
            src_ref=leaving.at[j], dst_ref=arrived.at[g],
            send_sem=tile_send.at[j], recv_sem=tile_recv.at[g],
            device_id={"occ": owner}, device_id_type=MESH,
        )
        copy.start()
        tile_copies.append(copy)

    for copy in inter_copies:
        copy.wait()

    def add(subtile, table, first, last):
        k = jnp.maximum(jnp.sum(jnp.where(table == g, label, 0)) - 1, 0)
        h, c = lax.div(k, col_tiles), lax.rem(k, col_tiles)
        part = jnp.dot(subtile, inter[c], preferred_element_type=jnp.float32)
        for i in range(halves):
            rows = pl.ds(i * SROWS, SROWS)
            term = jnp.where(h == i, part, 0.0)
            term = term if first else total[rows] + term
            if last:
                out_ref[rows] = term.astype(out_ref.dtype)
            else:
                total[rows] = term

    add(made(g), named, True, n_occ == 1)
    for j in reversed(range(n_occ - 1)):
        source = peer(g, j, n_occ)
        pltpu.make_async_remote_copy(
            src_ref=route, dst_ref=tables.at[source],
            send_sem=table_send.at[j], recv_sem=table_recv.at[source],
            device_id={"occ": source}, device_id_type=MESH,
        ).wait_recv()
        pltpu.make_async_remote_copy(
            src_ref=leaving.at[j], dst_ref=arrived.at[source],
            send_sem=tile_send.at[j], recv_sem=tile_recv.at[source],
            device_id={"occ": source}, device_id_type=MESH,
        ).wait_recv()
        add(arrived[source], tables[source, 0:1, 0:n_sub], False, j == 0)

    for key in crossing:
        crossing[key][0].wait_send()
    for key in pairing:
        pairing[key].wait_send()
    for copy in table_copies + tile_copies:
        copy.wait_send()


def solution(mesh):
    n_virt, n_occ = mesh.shape["virt"], mesh.shape["occ"]
    n_chips = n_virt // 2
    dims = n_chips.bit_length() - 1
    assert n_chips == 1 << dims

    def on_device(amplitudes, integrals, panel_owner, inter, dest, screen):
        op_rows, tile = amplitudes.shape
        w_cols = inter.shape[1]
        halves, col_tiles = op_rows // SROWS, integrals.shape[1] // tile
        return pl.pallas_call(
            functools.partial(kernel, n_virt, n_occ, dims),
            out_shape=jax.ShapeDtypeStruct((op_rows, w_cols), jnp.bfloat16),
            in_specs=[
                pl.BlockSpec(memory_space=pl.ANY),
            ] * 6,
            out_specs=pl.BlockSpec(memory_space=pltpu.VMEM),
            scratch_shapes=[
                pltpu.SMEM(panel_owner.shape, jnp.int32),
                pltpu.VMEM(dest.shape, jnp.int32),
                pltpu.VMEM(screen.shape, jnp.int32),
                pltpu.VMEM((n_virt, halves, SROWS, tile), jnp.bfloat16),
                pltpu.VMEM((col_tiles, integrals.shape[0], tile), jnp.bfloat16),
                pltpu.VMEM((col_tiles, tile, w_cols), jnp.bfloat16),
                pltpu.VMEM((8, 128), jnp.int32),
                pltpu.VMEM((n_occ, 8, 128), jnp.int32),
                pltpu.VMEM((n_occ, SROWS, tile), jnp.bfloat16),
                pltpu.VMEM((n_occ, SROWS, tile), jnp.bfloat16),
                pltpu.VMEM((op_rows, w_cols), jnp.float32),
                pltpu.SemaphoreType.DMA((3,)),
                pltpu.SemaphoreType.DMA,
                pltpu.SemaphoreType.DMA((col_tiles,)),
                pltpu.SemaphoreType.DMA((col_tiles,)),
                pltpu.SemaphoreType.REGULAR,
                pltpu.SemaphoreType.REGULAR,
                pltpu.SemaphoreType.DMA((dims, n_chips)),
                pltpu.SemaphoreType.DMA((dims, n_chips)),
                pltpu.SemaphoreType.DMA((dims, n_chips)),
                pltpu.SemaphoreType.DMA((dims, n_chips)),
                pltpu.SemaphoreType.DMA((n_occ,)),
                pltpu.SemaphoreType.DMA((n_occ,)),
                pltpu.SemaphoreType.DMA((n_occ,)),
                pltpu.SemaphoreType.DMA((n_occ,)),
            ],
            compiler_params=pltpu.CompilerParams(collective_id=0, has_side_effects=True, vmem_limit_bytes=24 << 20),
        )(*[pltpu.with_memory_space_constraint(x, pltpu.HBM) for x in (panel_owner, dest, screen, amplitudes.reshape(halves, SROWS, tile), integrals, inter)])

    return jax.shard_map(
        on_device,
        mesh=mesh,
        in_specs=(
            P("occ", "virt"),
            P(None, "virt"),
            P("occ", None),
            P("occ", "virt"),
            P("occ", "virt", None),
            P("occ", "virt", None),
        ),
        out_specs=P("occ", "virt"),
        check_vma=False,
    )
```

```python
import functools

import jax
import jax.numpy as jnp
from jax import lax
from jax.experimental import pallas as pl
from jax.experimental.pallas import tpu as pltpu
from jax.sharding import PartitionSpec as P

SROWS = 32
MESH = pl.DeviceIdType.MESH


def flip(index, bit):
    return index + bit * (1 - 2 * lax.rem(lax.div(index, bit), 2))


def peer(me, j, n):
    up = lax.div(me, (n + 1) // 2)
    rising = j + lax.div(j - me + n, n)
    falling = n - 1 - j
    falling = falling - lax.div(me - falling + n, n)
    return up * rising + (1 - up) * falling


def kernel(
    n_virt, n_occ, dims,
    owner_hbm, dest_hbm, screen_hbm, amp_hbm, integ_hbm, inter_hbm,
    out_ref,
    owner_ref, dest_ref, screen_ref, held, integ, inter, route, tables, leaving, arrived, total,
    small_sem, amp_sem, integ_sem, inter_sem, left_sem, right_sem,
    chip_send, chip_recv, pair_send, pair_recv,
    table_send, table_recv, tile_send, tile_recv,
):
    v = lax.axis_index("virt")
    g = lax.axis_index("occ")
    n_chips = n_virt // 2
    chip, core = lax.div(v, 2), lax.rem(v, 2)
    pair = flip(v, 1)
    halves, tile = held.shape[1], held.shape[3]
    steps = owner_ref.shape[1]
    n_sub = dest_ref.shape[2]
    col_tiles = integ.shape[0]

    barrier = pltpu.get_barrier_semaphore()
    pl.semaphore_signal(barrier, inc=1, device_id={"virt": pair}, device_id_type=MESH)
    for d in range(dims):
        near = flip(chip, 1 << d) * 2 + core
        pl.semaphore_signal(barrier, inc=1, device_id={"virt": near}, device_id_type=MESH)

    def to_right(sem):
        pl.semaphore_signal(sem, inc=1, device_id={"occ": lax.rem(g + 1, n_occ)}, device_id_type=MESH)

    def to_left(sem):
        pl.semaphore_signal(sem, inc=1, device_id={"occ": lax.rem(g + n_occ - 1, n_occ)}, device_id_type=MESH)

    @pl.when(g < n_occ - 1)
    def _():
        to_right(barrier)

    @pl.when(g > 0)
    def _():
        to_left(barrier)

    amp_copy = pltpu.make_async_copy(amp_hbm, held.at[v], amp_sem)
    amp_copy.start()
    small_copies = [
        pltpu.make_async_copy(src, dst, small_sem.at[i])
        for i, (src, dst) in enumerate(
            [(dest_hbm, dest_ref), (screen_hbm, screen_ref), (owner_hbm, owner_ref)]
        )
    ]
    for copy in small_copies:
        copy.start()

    def told_send(r):
        @pl.when((g >= r - 1) & (g < n_occ - 1))
        def _():
            to_right(left_sem)

        @pl.when((g <= n_occ - r) & (g > 0))
        def _():
            to_left(right_sem)

    def told_wait(r):
        @pl.when(g >= r)
        def _():
            pl.semaphore_wait(left_sem, 1)

        @pl.when(g <= n_occ - 1 - r)
        def _():
            pl.semaphore_wait(right_sem, 1)

    integ_copies, inter_copies = [], []
    for c in range(col_tiles):
        part = integ_hbm.at[:, pl.ds(c * tile, tile)]
        integ_copies.append(pltpu.make_async_copy(part, integ.at[c], integ_sem.at[c]))
        integ_copies[-1].start()

    for copy in small_copies:
        copy.wait()
    named = jnp.where(screen_ref[0] == 1, dest_ref[0], -1)
    route[...] = jnp.full(route.shape, -1, jnp.int32)
    route[0:1, 0:n_sub] = named
    label = lax.broadcasted_iota(jnp.int32, (1, n_sub), 1) + 1

    amp_copy.wait()
    below, above = lax.div(g + n_occ - 1, n_occ), lax.div(2 * n_occ - 2 - g, n_occ)
    pl.semaphore_wait(barrier, 1 + dims + below + above)

    parts = chip_recv.shape[0]
    part_halves = halves // parts

    def chunk(p, rel, bit_core):
        source = chip
        for d in range(dims):
            if rel >> d & 1:
                source = flip(source, 1 << d)
        return held.at[source * 2 + bit_core, pl.ds(p * part_halves, part_halves)]

    def chip_copy(p, rel, d):
        ref = chunk(p, rel, core)
        got = rel ^ (1 << d)
        return pltpu.make_async_remote_copy(
            src_ref=ref, dst_ref=ref,
            send_sem=chip_send.at[p, got], recv_sem=chip_recv.at[p, got],
            device_id={"virt": flip(chip, 1 << d) * 2 + core}, device_id_type=MESH,
        )

    def pair_copy(p, rel):
        ref = chunk(p, rel, core)
        return pltpu.make_async_remote_copy(
            src_ref=ref, dst_ref=ref,
            send_sem=pair_send.at[p, rel], recv_sem=pair_recv.at[p, rel],
            device_id={"virt": pair}, device_id_type=MESH,
        )

    orders = [[(p + t) % dims for t in range(dims)] for p in range(parts)]
    crossing, pairing = {}, {}

    def send_on(p, rel, first):
        for t in range(first, dims):
            d = orders[p][t]
            copy = chip_copy(p, rel, d)
            copy.start()
            crossing[p, rel ^ (1 << d)] = (copy, t + 1)

    for t in range(dims):
        for p in range(parts):
            d = orders[p][t]
            copy = chip_copy(p, 0, d)
            copy.start()
            crossing[p, 1 << d] = (copy, t + 1)
    for p in range(parts):
        pairing[p, 0] = pair_copy(p, 0)
        pairing[p, 0].start()

    if n_occ > 2:
        told_send(2)
    for c in range(col_tiles):
        part = inter_hbm.at[pl.ds(c * tile, tile)]
        inter_copies.append(pltpu.make_async_copy(part, inter.at[c], inter_sem.at[c]))
        inter_copies[-1].start()

    for depth in range(1, dims + 1):
        if depth == dims:
            for r in range(2, n_occ - 1):
                told_wait(r)
                told_send(r + 1)
        keys = [k for k in crossing if crossing[k][1] == depth]
        for key in sorted(keys, key=lambda k: (bin(k[1]).count("1"), k)):
            copy, after = crossing[key]
            copy.wait_recv()
            send_on(key[0], key[1], after)
            pairing[key] = pair_copy(*key)
            pairing[key].start()

    for key in pairing:
        pairing[key].wait_recv()

    for copy in integ_copies:
        copy.wait()
    if n_occ > 2:
        told_wait(n_occ - 1)

    table_copies = []
    for j in range(n_occ - 1):
        copy = pltpu.make_async_remote_copy(
            src_ref=route, dst_ref=tables.at[g],
            send_sem=table_send.at[j], recv_sem=table_recv.at[g],
            device_id={"occ": peer(g, j, n_occ)}, device_id_type=MESH,
        )
        copy.start()
        table_copies.append(copy)

    def made(owner):
        k1 = jnp.sum(jnp.where(named == owner, label, 0))
        k = jnp.maximum(k1 - 1, 0)
        h, c = lax.div(k, col_tiles), lax.rem(k, col_tiles)
        acc = jnp.zeros((SROWS, tile), jnp.float32)
        for s in range(steps):
            left = held[owner_ref[0, s], h]
            right = integ[c, pl.ds(s * tile, tile), :]
            acc += jnp.dot(left, right, preferred_element_type=jnp.float32)
        return jnp.where(k1 > 0, acc, 0.0).astype(jnp.bfloat16)

    tile_copies = []
    for j in range(n_occ - 1):
        owner = peer(g, j, n_occ)
        leaving[j] = made(owner)
        copy = pltpu.make_async_remote_copy(
            src_ref=leaving.at[j], dst_ref=arrived.at[g],
            send_sem=tile_send.at[j], recv_sem=tile_recv.at[g],
            device_id={"occ": owner}, device_id_type=MESH,
        )
        copy.start()
        tile_copies.append(copy)

    for copy in inter_copies:
        copy.wait()

    def add(subtile, table, first, last):
        k = jnp.maximum(jnp.sum(jnp.where(table == g, label, 0)) - 1, 0)
        h, c = lax.div(k, col_tiles), lax.rem(k, col_tiles)
        part = jnp.dot(subtile, inter[c], preferred_element_type=jnp.float32)
        for i in range(halves):
            rows = pl.ds(i * SROWS, SROWS)
            term = jnp.where(h == i, part, 0.0)
            term = term if first else total[rows] + term
            if last:
                out_ref[rows] = term.astype(out_ref.dtype)
            else:
                total[rows] = term

    add(made(g), named, True, n_occ == 1)
    for j in reversed(range(n_occ - 1)):
        source = peer(g, j, n_occ)
        pltpu.make_async_remote_copy(
            src_ref=route, dst_ref=tables.at[source],
            send_sem=table_send.at[j], recv_sem=table_recv.at[source],
            device_id={"occ": source}, device_id_type=MESH,
        ).wait_recv()
        pltpu.make_async_remote_copy(
            src_ref=leaving.at[j], dst_ref=arrived.at[source],
            send_sem=tile_send.at[j], recv_sem=tile_recv.at[source],
            device_id={"occ": source}, device_id_type=MESH,
        ).wait_recv()
        add(arrived[source], tables[source, 0:1, 0:n_sub], False, j == 0)

    for key in crossing:
        crossing[key][0].wait_send()
    for key in pairing:
        pairing[key].wait_send()
    for copy in table_copies + tile_copies:
        copy.wait_send()


def solution(mesh):
    n_virt, n_occ = mesh.shape["virt"], mesh.shape["occ"]
    n_chips = n_virt // 2
    dims = n_chips.bit_length() - 1
    assert n_chips == 1 << dims

    def on_device(amplitudes, integrals, panel_owner, inter, dest, screen):
        op_rows, tile = amplitudes.shape
        w_cols = inter.shape[1]
        halves, col_tiles = op_rows // SROWS, integrals.shape[1] // tile
        parts = halves if halves % dims == 0 else dims
        return pl.pallas_call(
            functools.partial(kernel, n_virt, n_occ, dims),
            out_shape=jax.ShapeDtypeStruct((op_rows, w_cols), jnp.bfloat16),
            in_specs=[
                pl.BlockSpec(memory_space=pl.ANY),
            ] * 6,
            out_specs=pl.BlockSpec(memory_space=pltpu.VMEM),
            scratch_shapes=[
                pltpu.SMEM(panel_owner.shape, jnp.int32),
                pltpu.VMEM(dest.shape, jnp.int32),
                pltpu.VMEM(screen.shape, jnp.int32),
                pltpu.VMEM((n_virt, halves, SROWS, tile), jnp.bfloat16),
                pltpu.VMEM((col_tiles, integrals.shape[0], tile), jnp.bfloat16),
                pltpu.VMEM((col_tiles, tile, w_cols), jnp.bfloat16),
                pltpu.VMEM((8, 128), jnp.int32),
                pltpu.VMEM((n_occ, 8, 128), jnp.int32),
                pltpu.VMEM((n_occ, SROWS, tile), jnp.bfloat16),
                pltpu.VMEM((n_occ, SROWS, tile), jnp.bfloat16),
                pltpu.VMEM((op_rows, w_cols), jnp.float32),
                pltpu.SemaphoreType.DMA((3,)),
                pltpu.SemaphoreType.DMA,
                pltpu.SemaphoreType.DMA((col_tiles,)),
                pltpu.SemaphoreType.DMA((col_tiles,)),
                pltpu.SemaphoreType.REGULAR,
                pltpu.SemaphoreType.REGULAR,
                pltpu.SemaphoreType.DMA((parts, n_chips)),
                pltpu.SemaphoreType.DMA((parts, n_chips)),
                pltpu.SemaphoreType.DMA((parts, n_chips)),
                pltpu.SemaphoreType.DMA((parts, n_chips)),
                pltpu.SemaphoreType.DMA((n_occ,)),
                pltpu.SemaphoreType.DMA((n_occ,)),
                pltpu.SemaphoreType.DMA((n_occ,)),
                pltpu.SemaphoreType.DMA((n_occ,)),
            ],
            compiler_params=pltpu.CompilerParams(collective_id=0, has_side_effects=True, vmem_limit_bytes=24 << 20),
        )(*[pltpu.with_memory_space_constraint(x, pltpu.HBM) for x in (panel_owner, dest, screen, amplitudes.reshape(halves, SROWS, tile), integrals, inter)])

    return jax.shard_map(
        on_device,
        mesh=mesh,
        in_specs=(
            P("occ", "virt"),
            P(None, "virt"),
            P("occ", None),
            P("occ", "virt"),
            P("occ", "virt", None),
            P("occ", "virt", None),
        ),
        out_specs=P("occ", "virt"),
        check_vma=False,
    )
```

```python
import functools

import jax
import jax.numpy as jnp
from jax import lax
from jax.experimental import pallas as pl
from jax.experimental.pallas import tpu as pltpu
from jax.sharding import PartitionSpec as P

SROWS = 32
MESH = pl.DeviceIdType.MESH


def flip(index, bit):
    return index + bit * (1 - 2 * lax.rem(lax.div(index, bit), 2))


def peer(me, j, n):
    up = lax.div(me, (n + 1) // 2)
    rising = j + lax.div(j - me + n, n)
    falling = n - 1 - j
    falling = falling - lax.div(me - falling + n, n)
    return up * rising + (1 - up) * falling


def kernel(
    n_virt, n_occ, dims,
    owner_hbm, dest_hbm, screen_hbm, amp_hbm, integ_hbm, inter_hbm,
    out_ref,
    owner_ref, dest_ref, screen_ref, held, integ, inter, route, tables, leaving, arrived, total,
    small_sem, amp_sem, integ_sem, inter_sem, left_sem, right_sem,
    chip_send, chip_recv, pair_send, pair_recv,
    table_send, table_recv, tile_send, tile_recv,
):
    v = lax.axis_index("virt")
    g = lax.axis_index("occ")
    n_chips = n_virt // 2
    chip, core = lax.div(v, 2), lax.rem(v, 2)
    pair = flip(v, 1)
    halves, tile = held.shape[1], held.shape[3]
    steps = owner_ref.shape[1]
    n_sub = dest_ref.shape[2]
    col_tiles = integ.shape[0]

    barrier = pltpu.get_barrier_semaphore()
    pl.semaphore_signal(barrier, inc=1, device_id={"virt": pair}, device_id_type=MESH)
    for d in range(dims):
        near = flip(chip, 1 << d) * 2 + core
        pl.semaphore_signal(barrier, inc=1, device_id={"virt": near}, device_id_type=MESH)

    def to_right(sem):
        pl.semaphore_signal(sem, inc=1, device_id={"occ": lax.rem(g + 1, n_occ)}, device_id_type=MESH)

    def to_left(sem):
        pl.semaphore_signal(sem, inc=1, device_id={"occ": lax.rem(g + n_occ - 1, n_occ)}, device_id_type=MESH)

    @pl.when(g < n_occ - 1)
    def _():
        to_right(barrier)

    @pl.when(g > 0)
    def _():
        to_left(barrier)

    amp_copy = pltpu.make_async_copy(amp_hbm, held.at[v], amp_sem)
    amp_copy.start()

    def told_send(r):
        @pl.when((g >= r - 1) & (g < n_occ - 1))
        def _():
            to_right(left_sem)

        @pl.when((g <= n_occ - r) & (g > 0))
        def _():
            to_left(right_sem)

    def told_wait(r):
        @pl.when(g >= r)
        def _():
            pl.semaphore_wait(left_sem, 1)

        @pl.when(g <= n_occ - 1 - r)
        def _():
            pl.semaphore_wait(right_sem, 1)

    integ_copies, inter_copies = [], []

    amp_copy.wait()
    below, above = lax.div(g + n_occ - 1, n_occ), lax.div(2 * n_occ - 2 - g, n_occ)
    pl.semaphore_wait(barrier, 1 + dims + below + above)

    parts = chip_recv.shape[0]
    part_halves = halves // parts

    def chunk(p, rel, bit_core):
        source = chip
        for d in range(dims):
            if rel >> d & 1:
                source = flip(source, 1 << d)
        return held.at[source * 2 + bit_core, pl.ds(p * part_halves, part_halves)]

    def chip_copy(p, rel, d):
        ref = chunk(p, rel, core)
        got = rel ^ (1 << d)
        return pltpu.make_async_remote_copy(
            src_ref=ref, dst_ref=ref,
            send_sem=chip_send.at[p, got], recv_sem=chip_recv.at[p, got],
            device_id={"virt": flip(chip, 1 << d) * 2 + core}, device_id_type=MESH,
        )

    def pair_copy(p, rel):
        ref = chunk(p, rel, core)
        return pltpu.make_async_remote_copy(
            src_ref=ref, dst_ref=ref,
            send_sem=pair_send.at[p, rel], recv_sem=pair_recv.at[p, rel],
            device_id={"virt": pair}, device_id_type=MESH,
        )

    orders = [[(p + t) % dims for t in range(dims)] for p in range(parts)]
    crossing, pairing = {}, {}

    def send_on(p, rel, first):
        for t in range(first, dims):
            d = orders[p][t]
            copy = chip_copy(p, rel, d)
            copy.start()
            crossing[p, rel ^ (1 << d)] = (copy, t + 1)

    for t in range(dims):
        for p in range(parts):
            d = orders[p][t]
            copy = chip_copy(p, 0, d)
            copy.start()
            crossing[p, 1 << d] = (copy, t + 1)
    for p in range(parts):
        pairing[p, 0] = pair_copy(p, 0)
        pairing[p, 0].start()

    if n_occ > 2:
        told_send(2)
    small_copies = [
        pltpu.make_async_copy(src, dst, small_sem.at[i])
        for i, (src, dst) in enumerate(
            [(dest_hbm, dest_ref), (screen_hbm, screen_ref), (owner_hbm, owner_ref)]
        )
    ]
    for copy in small_copies:
        copy.start()
    for c in range(col_tiles):
        part = integ_hbm.at[:, pl.ds(c * tile, tile)]
        integ_copies.append(pltpu.make_async_copy(part, integ.at[c], integ_sem.at[c]))
        integ_copies[-1].start()
    for c in range(col_tiles):
        part = inter_hbm.at[pl.ds(c * tile, tile)]
        inter_copies.append(pltpu.make_async_copy(part, inter.at[c], inter_sem.at[c]))
        inter_copies[-1].start()

    for copy in small_copies:
        copy.wait()
    named = jnp.where(screen_ref[0] == 1, dest_ref[0], -1)
    route[...] = jnp.full(route.shape, -1, jnp.int32)
    route[0:1, 0:n_sub] = named
    label = lax.broadcasted_iota(jnp.int32, (1, n_sub), 1) + 1

    for depth in range(1, dims + 1):
        if depth == dims:
            for r in range(2, n_occ - 1):
                told_wait(r)
                told_send(r + 1)
        keys = [k for k in crossing if crossing[k][1] == depth]
        for key in sorted(keys, key=lambda k: (bin(k[1]).count("1"), k)):
            copy, after = crossing[key]
            copy.wait_recv()
            send_on(key[0], key[1], after)
            pairing[key] = pair_copy(*key)
            pairing[key].start()

    for key in pairing:
        pairing[key].wait_recv()

    for copy in integ_copies:
        copy.wait()
    if n_occ > 2:
        told_wait(n_occ - 1)

    table_copies = []
    for j in range(n_occ - 1):
        copy = pltpu.make_async_remote_copy(
            src_ref=route, dst_ref=tables.at[g],
            send_sem=table_send.at[j], recv_sem=table_recv.at[g],
            device_id={"occ": peer(g, j, n_occ)}, device_id_type=MESH,
        )
        copy.start()
        table_copies.append(copy)

    def made(owner):
        k1 = jnp.sum(jnp.where(named == owner, label, 0))
        k = jnp.maximum(k1 - 1, 0)
        h, c = lax.div(k, col_tiles), lax.rem(k, col_tiles)
        acc = jnp.zeros((SROWS, tile), jnp.float32)
        for s in range(steps):
            left = held[owner_ref[0, s], h]
            right = integ[c, pl.ds(s * tile, tile), :]
            acc += jnp.dot(left, right, preferred_element_type=jnp.float32)
        return jnp.where(k1 > 0, acc, 0.0).astype(jnp.bfloat16)

    tile_copies = []
    for j in range(n_occ - 1):
        owner = peer(g, j, n_occ)
        leaving[j] = made(owner)
        copy = pltpu.make_async_remote_copy(
            src_ref=leaving.at[j], dst_ref=arrived.at[g],
            send_sem=tile_send.at[j], recv_sem=tile_recv.at[g],
            device_id={"occ": owner}, device_id_type=MESH,
        )
        copy.start()
        tile_copies.append(copy)

    for copy in inter_copies:
        copy.wait()

    def add(subtile, table, first, last):
        k = jnp.maximum(jnp.sum(jnp.where(table == g, label, 0)) - 1, 0)
        h, c = lax.div(k, col_tiles), lax.rem(k, col_tiles)
        part = jnp.dot(subtile, inter[c], preferred_element_type=jnp.float32)
        for i in range(halves):
            rows = pl.ds(i * SROWS, SROWS)
            term = jnp.where(h == i, part, 0.0)
            term = term if first else total[rows] + term
            if last:
                out_ref[rows] = term.astype(out_ref.dtype)
            else:
                total[rows] = term

    add(made(g), named, True, n_occ == 1)
    for j in reversed(range(n_occ - 1)):
        source = peer(g, j, n_occ)
        pltpu.make_async_remote_copy(
            src_ref=route, dst_ref=tables.at[source],
            send_sem=table_send.at[j], recv_sem=table_recv.at[source],
            device_id={"occ": source}, device_id_type=MESH,
        ).wait_recv()
        pltpu.make_async_remote_copy(
            src_ref=leaving.at[j], dst_ref=arrived.at[source],
            send_sem=tile_send.at[j], recv_sem=tile_recv.at[source],
            device_id={"occ": source}, device_id_type=MESH,
        ).wait_recv()
        add(arrived[source], tables[source, 0:1, 0:n_sub], False, j == 0)

    for key in crossing:
        crossing[key][0].wait_send()
    for key in pairing:
        pairing[key].wait_send()
    for copy in table_copies + tile_copies:
        copy.wait_send()


def solution(mesh):
    n_virt, n_occ = mesh.shape["virt"], mesh.shape["occ"]
    n_chips = n_virt // 2
    dims = n_chips.bit_length() - 1
    assert n_chips == 1 << dims

    def on_device(amplitudes, integrals, panel_owner, inter, dest, screen):
        op_rows, tile = amplitudes.shape
        w_cols = inter.shape[1]
        halves, col_tiles = op_rows // SROWS, integrals.shape[1] // tile
        parts = halves if halves % dims == 0 else dims
        return pl.pallas_call(
            functools.partial(kernel, n_virt, n_occ, dims),
            out_shape=jax.ShapeDtypeStruct((op_rows, w_cols), jnp.bfloat16),
            in_specs=[
                pl.BlockSpec(memory_space=pl.ANY),
            ] * 6,
            out_specs=pl.BlockSpec(memory_space=pltpu.VMEM),
            scratch_shapes=[
                pltpu.SMEM(panel_owner.shape, jnp.int32),
                pltpu.VMEM(dest.shape, jnp.int32),
                pltpu.VMEM(screen.shape, jnp.int32),
                pltpu.VMEM((n_virt, halves, SROWS, tile), jnp.bfloat16),
                pltpu.VMEM((col_tiles, integrals.shape[0], tile), jnp.bfloat16),
                pltpu.VMEM((col_tiles, tile, w_cols), jnp.bfloat16),
                pltpu.VMEM((8, 128), jnp.int32),
                pltpu.VMEM((n_occ, 8, 128), jnp.int32),
                pltpu.VMEM((n_occ, SROWS, tile), jnp.bfloat16),
                pltpu.VMEM((n_occ, SROWS, tile), jnp.bfloat16),
                pltpu.VMEM((op_rows, w_cols), jnp.float32),
                pltpu.SemaphoreType.DMA((3,)),
                pltpu.SemaphoreType.DMA,
                pltpu.SemaphoreType.DMA((col_tiles,)),
                pltpu.SemaphoreType.DMA((col_tiles,)),
                pltpu.SemaphoreType.REGULAR,
                pltpu.SemaphoreType.REGULAR,
                pltpu.SemaphoreType.DMA((parts, n_chips)),
                pltpu.SemaphoreType.DMA((parts, n_chips)),
                pltpu.SemaphoreType.DMA((parts, n_chips)),
                pltpu.SemaphoreType.DMA((parts, n_chips)),
                pltpu.SemaphoreType.DMA((n_occ,)),
                pltpu.SemaphoreType.DMA((n_occ,)),
                pltpu.SemaphoreType.DMA((n_occ,)),
                pltpu.SemaphoreType.DMA((n_occ,)),
            ],
            compiler_params=pltpu.CompilerParams(collective_id=0, has_side_effects=True, vmem_limit_bytes=24 << 20),
        )(*[pltpu.with_memory_space_constraint(x, pltpu.HBM) for x in (panel_owner, dest, screen, amplitudes.reshape(halves, SROWS, tile), integrals, inter)])

    return jax.shard_map(
        on_device,
        mesh=mesh,
        in_specs=(
            P("occ", "virt"),
            P(None, "virt"),
            P("occ", None),
            P("occ", "virt"),
            P("occ", "virt", None),
            P("occ", "virt", None),
        ),
        out_specs=P("occ", "virt"),
        check_vma=False,
    )
```

```python
import functools

import jax
import jax.numpy as jnp
from jax import lax
from jax.experimental import pallas as pl
from jax.experimental.pallas import tpu as pltpu
from jax.sharding import PartitionSpec as P

SROWS = 32
MESH = pl.DeviceIdType.MESH


def flip(index, bit):
    return index + bit * (1 - 2 * lax.rem(lax.div(index, bit), 2))


def peer(me, j, n):
    up = lax.div(me, (n + 1) // 2)
    rising = j + lax.div(j - me + n, n)
    falling = n - 1 - j
    falling = falling - lax.div(me - falling + n, n)
    return up * rising + (1 - up) * falling


def kernel(
    n_virt, n_occ, dims,
    owner_hbm, dest_hbm, screen_hbm, amp_hbm, integ_hbm, inter_hbm,
    out_ref,
    owner_ref, dest_ref, screen_ref, held, integ, inter, route, tables, leaving, arrived, total,
    small_sem, amp_sem, integ_sem, inter_sem, left_sem, right_sem,
    chip_send, chip_recv, pair_send, pair_recv,
    table_send, table_recv, tile_send, tile_recv,
):
    v = lax.axis_index("virt")
    g = lax.axis_index("occ")
    n_chips = n_virt // 2
    chip, core = lax.div(v, 2), lax.rem(v, 2)
    pair = flip(v, 1)
    halves, tile = held.shape[1], held.shape[3]
    steps = owner_ref.shape[1]
    n_sub = dest_ref.shape[2]
    col_tiles = integ.shape[0]

    barrier = pltpu.get_barrier_semaphore()
    pl.semaphore_signal(barrier, inc=1, device_id={"virt": pair}, device_id_type=MESH)
    for d in range(dims):
        near = flip(chip, 1 << d) * 2 + core
        pl.semaphore_signal(barrier, inc=1, device_id={"virt": near}, device_id_type=MESH)

    def to_right(sem):
        pl.semaphore_signal(sem, inc=1, device_id={"occ": lax.rem(g + 1, n_occ)}, device_id_type=MESH)

    def to_left(sem):
        pl.semaphore_signal(sem, inc=1, device_id={"occ": lax.rem(g + n_occ - 1, n_occ)}, device_id_type=MESH)

    @pl.when(g < n_occ - 1)
    def _():
        to_right(barrier)

    @pl.when(g > 0)
    def _():
        to_left(barrier)

    amp_copy = pltpu.make_async_copy(amp_hbm, held.at[v], amp_sem)
    amp_copy.start()

    def told_send(r):
        @pl.when((g >= r - 1) & (g < n_occ - 1))
        def _():
            to_right(left_sem)

        @pl.when((g <= n_occ - r) & (g > 0))
        def _():
            to_left(right_sem)

    def told_wait(r):
        @pl.when(g >= r)
        def _():
            pl.semaphore_wait(left_sem, 1)

        @pl.when(g <= n_occ - 1 - r)
        def _():
            pl.semaphore_wait(right_sem, 1)

    integ_copies, inter_copies = [], []

    amp_copy.wait()
    below, above = lax.div(g + n_occ - 1, n_occ), lax.div(2 * n_occ - 2 - g, n_occ)
    pl.semaphore_wait(barrier, 1 + dims + below + above)

    parts = chip_recv.shape[0]
    part_halves = halves // parts

    def chunk(p, rel, bit_core):
        source = chip
        for d in range(dims):
            if rel >> d & 1:
                source = flip(source, 1 << d)
        return held.at[source * 2 + bit_core, pl.ds(p * part_halves, part_halves)]

    def chip_copy(p, rel, d):
        ref = chunk(p, rel, core)
        got = rel ^ (1 << d)
        return pltpu.make_async_remote_copy(
            src_ref=ref, dst_ref=ref,
            send_sem=chip_send.at[p, got], recv_sem=chip_recv.at[p, got],
            device_id={"virt": flip(chip, 1 << d) * 2 + core}, device_id_type=MESH,
        )

    def pair_copy(p, rel):
        ref = chunk(p, rel, core)
        return pltpu.make_async_remote_copy(
            src_ref=ref, dst_ref=ref,
            send_sem=pair_send.at[p, rel], recv_sem=pair_recv.at[p, rel],
            device_id={"virt": pair}, device_id_type=MESH,
        )

    orders = [[(p + t) % dims for t in range(dims)] for p in range(parts)]
    crossing, pairing = {}, {}

    def send_on(p, rel, first):
        for t in range(first, dims):
            d = orders[p][t]
            copy = chip_copy(p, rel, d)
            copy.start()
            crossing[p, rel ^ (1 << d)] = (copy, t + 1)

    for t in range(dims):
        for p in range(parts):
            d = orders[p][t]
            copy = chip_copy(p, 0, d)
            copy.start()
            crossing[p, 1 << d] = (copy, t + 1)
    for p in range(parts):
        pairing[p, 0] = pair_copy(p, 0)
        pairing[p, 0].start()

    if n_occ > 2:
        told_send(2)
    small_copies = [
        pltpu.make_async_copy(src, dst, small_sem.at[i])
        for i, (src, dst) in enumerate(
            [(dest_hbm, dest_ref), (screen_hbm, screen_ref), (owner_hbm, owner_ref)]
        )
    ]
    for copy in small_copies:
        copy.start()
    for c in range(col_tiles):
        part = integ_hbm.at[:, pl.ds(c * tile, tile)]
        integ_copies.append(pltpu.make_async_copy(part, integ.at[c], integ_sem.at[c]))
        integ_copies[-1].start()
    for c in range(col_tiles):
        part = inter_hbm.at[pl.ds(c * tile, tile)]
        inter_copies.append(pltpu.make_async_copy(part, inter.at[c], inter_sem.at[c]))
        inter_copies[-1].start()

    for copy in small_copies:
        copy.wait()
    named = jnp.where(screen_ref[0] == 1, dest_ref[0], -1)
    route[...] = jnp.full(route.shape, -1, jnp.int32)
    route[0:1, 0:n_sub] = named
    label = lax.broadcasted_iota(jnp.int32, (1, n_sub), 1) + 1

    def label_for(table, owner):
        return jnp.sum(jnp.where(table == owner, label, 0))

    others = [label_for(named, peer(g, j, n_occ)) for j in range(n_occ - 1)]
    mine = label_for(named, g)

    for depth in range(1, dims + 1):
        if depth == dims:
            for r in range(2, n_occ - 1):
                told_wait(r)
                told_send(r + 1)
        keys = [k for k in crossing if crossing[k][1] == depth]
        for key in sorted(keys, key=lambda k: (bin(k[1]).count("1"), k)):
            copy, after = crossing[key]
            copy.wait_recv()
            send_on(key[0], key[1], after)
            pairing[key] = pair_copy(*key)
            pairing[key].start()

    for key in pairing:
        pairing[key].wait_recv()

    for copy in integ_copies:
        copy.wait()
    if n_occ > 2:
        told_wait(n_occ - 1)

    table_copies = []
    for j in range(n_occ - 1):
        copy = pltpu.make_async_remote_copy(
            src_ref=route, dst_ref=tables.at[g],
            send_sem=table_send.at[j], recv_sem=table_recv.at[g],
            device_id={"occ": peer(g, j, n_occ)}, device_id_type=MESH,
        )
        copy.start()
        table_copies.append(copy)

    def made(k1):
        k = jnp.maximum(k1 - 1, 0)
        h, c = lax.div(k, col_tiles), lax.rem(k, col_tiles)
        acc = jnp.zeros((SROWS, tile), jnp.float32)
        for s in range(steps):
            left = held[owner_ref[0, s], h]
            right = integ[c, pl.ds(s * tile, tile), :]
            acc += jnp.dot(left, right, preferred_element_type=jnp.float32)
        return jnp.where(k1 > 0, acc, 0.0).astype(jnp.bfloat16)

    tile_copies = []
    for j in range(n_occ - 1):
        owner = peer(g, j, n_occ)
        leaving[j] = made(others[j])
        copy = pltpu.make_async_remote_copy(
            src_ref=leaving.at[j], dst_ref=arrived.at[g],
            send_sem=tile_send.at[j], recv_sem=tile_recv.at[g],
            device_id={"occ": owner}, device_id_type=MESH,
        )
        copy.start()
        tile_copies.append(copy)

    for copy in inter_copies:
        copy.wait()

    def add(subtile, k1, first, last):
        k = jnp.maximum(k1 - 1, 0)
        h, c = lax.div(k, col_tiles), lax.rem(k, col_tiles)
        part = jnp.dot(subtile, inter[c], preferred_element_type=jnp.float32)
        for i in range(halves):
            rows = pl.ds(i * SROWS, SROWS)
            term = jnp.where(h == i, part, 0.0)
            term = term if first else total[rows] + term
            if last:
                out_ref[rows] = term.astype(out_ref.dtype)
            else:
                total[rows] = term

    add(made(mine), mine, True, n_occ == 1)
    for j in reversed(range(n_occ - 1)):
        source = peer(g, j, n_occ)
        pltpu.make_async_remote_copy(
            src_ref=route, dst_ref=tables.at[source],
            send_sem=table_send.at[j], recv_sem=table_recv.at[source],
            device_id={"occ": source}, device_id_type=MESH,
        ).wait_recv()
        k1 = label_for(tables[source, 0:1, 0:n_sub], g)
        pltpu.make_async_remote_copy(
            src_ref=leaving.at[j], dst_ref=arrived.at[source],
            send_sem=tile_send.at[j], recv_sem=tile_recv.at[source],
            device_id={"occ": source}, device_id_type=MESH,
        ).wait_recv()
        add(arrived[source], k1, False, j == 0)

    for key in crossing:
        crossing[key][0].wait_send()
    for key in pairing:
        pairing[key].wait_send()
    for copy in table_copies + tile_copies:
        copy.wait_send()


def solution(mesh):
    n_virt, n_occ = mesh.shape["virt"], mesh.shape["occ"]
    n_chips = n_virt // 2
    dims = n_chips.bit_length() - 1
    assert n_chips == 1 << dims

    def on_device(amplitudes, integrals, panel_owner, inter, dest, screen):
        op_rows, tile = amplitudes.shape
        w_cols = inter.shape[1]
        halves, col_tiles = op_rows // SROWS, integrals.shape[1] // tile
        parts = halves if halves % dims == 0 else dims
        return pl.pallas_call(
            functools.partial(kernel, n_virt, n_occ, dims),
            out_shape=jax.ShapeDtypeStruct((op_rows, w_cols), jnp.bfloat16),
            in_specs=[
                pl.BlockSpec(memory_space=pl.ANY),
            ] * 6,
            out_specs=pl.BlockSpec(memory_space=pltpu.VMEM),
            scratch_shapes=[
                pltpu.SMEM(panel_owner.shape, jnp.int32),
                pltpu.VMEM(dest.shape, jnp.int32),
                pltpu.VMEM(screen.shape, jnp.int32),
                pltpu.VMEM((n_virt, halves, SROWS, tile), jnp.bfloat16),
                pltpu.VMEM((col_tiles, integrals.shape[0], tile), jnp.bfloat16),
                pltpu.VMEM((col_tiles, tile, w_cols), jnp.bfloat16),
                pltpu.VMEM((8, 128), jnp.int32),
                pltpu.VMEM((n_occ, 8, 128), jnp.int32),
                pltpu.VMEM((n_occ, SROWS, tile), jnp.bfloat16),
                pltpu.VMEM((n_occ, SROWS, tile), jnp.bfloat16),
                pltpu.VMEM((op_rows, w_cols), jnp.float32),
                pltpu.SemaphoreType.DMA((3,)),
                pltpu.SemaphoreType.DMA,
                pltpu.SemaphoreType.DMA((col_tiles,)),
                pltpu.SemaphoreType.DMA((col_tiles,)),
                pltpu.SemaphoreType.REGULAR,
                pltpu.SemaphoreType.REGULAR,
                pltpu.SemaphoreType.DMA((parts, n_chips)),
                pltpu.SemaphoreType.DMA((parts, n_chips)),
                pltpu.SemaphoreType.DMA((parts, n_chips)),
                pltpu.SemaphoreType.DMA((parts, n_chips)),
                pltpu.SemaphoreType.DMA((n_occ,)),
                pltpu.SemaphoreType.DMA((n_occ,)),
                pltpu.SemaphoreType.DMA((n_occ,)),
                pltpu.SemaphoreType.DMA((n_occ,)),
            ],
            compiler_params=pltpu.CompilerParams(collective_id=0, has_side_effects=True, vmem_limit_bytes=24 << 20),
        )(*[pltpu.with_memory_space_constraint(x, pltpu.HBM) for x in (panel_owner, dest, screen, amplitudes.reshape(halves, SROWS, tile), integrals, inter)])

    return jax.shard_map(
        on_device,
        mesh=mesh,
        in_specs=(
            P("occ", "virt"),
            P(None, "virt"),
            P("occ", None),
            P("occ", "virt"),
            P("occ", "virt", None),
            P("occ", "virt", None),
        ),
        out_specs=P("occ", "virt"),
        check_vma=False,
    )
```
